32 devices in a mesh: ctx: 16 (over z, x, core), head: 2 (over y).
Axes of the slice: x: 2, y: 2, z: 4, core: 2. Of those that a mesh axis runs over, the one named last changes fastest.
Arguments:
- q_nope: bfloat16 [2048, 16384], P('ctx', 'head'), may hold values from -6 to 6
- q_rope: bfloat16 [2048, 8192], P('ctx', 'head'), may hold values from -32 to 32
- latent: bfloat16 [2048, 576], P(('ctx', 'head')), may hold values from -32 to 32
- block_start: int32 [32], replicated, may hold values from 0 to 1984, as said below
- w_uk: bfloat16 [128, 128, 512], P('head'), may hold values from -0.5 to 0.5
- w_uv: bfloat16 [128, 512, 128], P('head'), may hold values from -1.5 to 1.5
Outputs:
- attn_out: bfloat16 [2048, 16384], P('ctx', 'head')
The draws below stay inside these ranges and needn't reach their ends.
Inputs may be any that keep to these rules, and one draw needn't show every extreme that they name: `block_start`: blocks 2 i and 2 i + 1 start at k * 64 and (31 - k) * 64 for a k that takes each value 0 to 15 once over i.
All inputs are finite; a program needn't handle non-finite values.
Results may differ from the reference program's by a relative error of at most 0.0065.
Values may be sent and summed in bfloat16 or wider, within the bound.
A program may use at most 192 MiB of HBM per device.

```python
import math
import jax
import jax.numpy as jnp
from jax import lax

HEADS = 128
DN = 128
DR = 64
LAT = 512
DV = 128
BLK = 64
SEQ = 2048
NBLK = 32


def draw_latent(key, part):
    own_key = jax.random.fold_in(key, 1)
    result = jnp.clip(jax.random.normal(own_key, (SEQ, LAT + DR), jnp.float32), -6.0, 6.0)
    return result.astype(jnp.bfloat16)


def draw_q_rope(key, part):
    own_key = jax.random.fold_in(key, 2)
    result = jnp.clip(jax.random.normal(own_key, (SEQ, HEADS * DR), jnp.float32), -6.0, 6.0)
    return result.astype(jnp.bfloat16)


def draw_block_start(key, part):
    order = jax.random.permutation(jax.random.fold_in(key, 3), NBLK // 2).astype(jnp.int32)
    lower_start = order * BLK
    upper_start = (NBLK - 1 - order) * BLK
    return jnp.stack([lower_start, upper_start], axis=1).reshape(NBLK).astype(jnp.int32)


def levels(key, dims, split, smallest, high):
    level, own = 1.0, jax.random.fold_in(key, 6)
    for axis_at, parts in split:
        heights = jnp.exp(jax.random.uniform(jax.random.fold_in(own, axis_at), (parts,), jnp.float32, smallest / len(split), high / len(split)))
        level = level * jnp.repeat(heights, dims[axis_at] // parts).reshape([-1 if axis == axis_at else 1 for axis in range(len(dims))])
    return level


def gaussian(key, shape, width, limit, split=(), kind=jnp.bfloat16):
    drawn = width * jax.random.normal(key, shape, jnp.float32)
    if split:
        drawn = drawn * levels(key, shape, split, -0.22, 0.18)
    return jnp.clip(drawn, -limit, limit).astype(kind)


def setup_inputs(seed: int = 0) -> dict:
    splits = jax.random.split(jax.random.key(seed), 7)
    q_nope = gaussian(splits[0], (SEQ, HEADS * DN), 1.0, 6.0, ((0, 16), (1, 2)))
    q_rope = draw_q_rope(jax.random.fold_in(splits[6], 71), 0)
    latent = draw_latent(jax.random.fold_in(splits[6], 71), 0)
    block_start = draw_block_start(jax.random.fold_in(splits[6], 71), 0)
    w_uk = gaussian(splits[4], (HEADS, DN, LAT), DN ** -0.5, 0.5, ((0, 2),))
    w_uv = gaussian(splits[5], (HEADS, LAT, DV), 0.25, 1.5, ((0, 2),))
    return dict(q_nope=q_nope, q_rope=q_rope, latent=latent, block_start=block_start, w_uk=w_uk, w_uv=w_uv)


def reference(q_nope, q_rope, latent, block_start, w_uk, w_uv):
    rows = jnp.arange(SEQ, dtype=jnp.int32)
    positions_all = jnp.take(block_start, rows // BLK) + rows % BLK
    allowed = positions_all[None, :] <= positions_all[:, None]
    score_scale = 1.0 / math.sqrt(DN + DR)
    nope_heads = q_nope.reshape(SEQ, HEADS, DN)
    rope_heads = q_rope.reshape(SEQ, HEADS, DR)

    def one_head(head_index):
        q_lat = jnp.dot(nope_heads[:, head_index, :], w_uk[head_index], preferred_element_type=jnp.float32).astype(jnp.bfloat16)
        query = jnp.concatenate([q_lat, rope_heads[:, head_index, :]], axis=1)
        scores = jnp.dot(query, latent.T, preferred_element_type=jnp.float32) * score_scale
        top_score = lax.optimization_barrier(jnp.max(jnp.where(allowed, scores, -1e+30), axis=1, keepdims=True))
        weights = jnp.where(allowed, jnp.exp(scores - top_score), 0.0)
        total = lax.optimization_barrier(jnp.sum(weights, axis=1, keepdims=True))
        o_lat = (jnp.dot(weights.astype(jnp.bfloat16), latent[:, :LAT], preferred_element_type=jnp.float32) / total).astype(jnp.bfloat16)
        return jnp.dot(o_lat, w_uv[head_index], preferred_element_type=jnp.float32).astype(jnp.bfloat16)
    outputs = lax.map(one_head, jnp.arange(HEADS, dtype=jnp.int32))
    return jnp.transpose(outputs, (1, 0, 2)).reshape(SEQ, HEADS * DV)
```

```python
import functools
import math

import jax
import jax.numpy as jnp
from jax import lax
from jax.experimental import pallas as pl
from jax.experimental.pallas import tpu as pltpu
from jax.sharding import PartitionSpec as P

CHUNK = 256
LANES = 128
GROUP = 16
UNIT = 8
TURN = 3
MESH = pl.DeviceIdType.MESH


def attention_kernel(
    scale2,
    blk,
    starts_ref,
    lat_ref,
    q_ref,
    wuv_ref,
    out_ref,
    lat_s,
    sc_s,
    acc_s,
    max_s,
    top_s,
    sum_s,
):
    group, width, value = wuv_ref.shape
    rows = group * blk
    seq, full = lat_ref.shape
    steps = seq // CHUNK + 1
    padded = lat_s.shape[1]
    me = lax.axis_index("ctx")
    start_a = starts_ref[2 * me]
    start_b = starts_ref[2 * me + 1]
    count_a = start_a // CHUNK + 1
    step = pl.program_id(0)
    last = pl.num_programs(0) - 1

    @pl.when(step == 0)
    def _():
        max_s[...] = jnp.full(max_s.shape, -1e30, jnp.float32)
        sum_s[...] = jnp.zeros(sum_s.shape, jnp.float32)
        acc_s[...] = jnp.zeros(acc_s.shape, jnp.float32)

        def place(b, _):
            src = pl.ds(pl.multiple_of(b * blk, blk), blk)
            dst = pl.ds(pl.multiple_of(starts_ref[b], blk), blk)
            lat_s[dst, :width] = lat_ref[src, :width]
            tail = lat_ref[src, width:]
            fill = jnp.zeros((blk, padded - full), tail.dtype)
            lat_s[dst, width:] = jnp.concatenate([tail, fill], axis=1)
            return 0

        lax.fori_loop(0, seq // blk, place, 0)

    def locate(t):
        upper = t >= count_a
        half = jnp.where(upper, 1, 0)
        chunk = jnp.where(upper, t - count_a, t)
        offset = jnp.where(upper, start_b, start_a) - chunk * CHUNK
        return half, pl.ds(pl.multiple_of(chunk * CHUNK, CHUNK), CHUNK), offset

    def weigh(t):
        half, keys, _ = locate(t)
        top = top_s[half]
        total = sum_s[half]
        pieces = []
        for j in range(CHUNK // LANES):
            w = jnp.exp2((sc_s[t, :, j * LANES : (j + 1) * LANES] - top) * scale2)
            total = total + w
            pieces.append(w.astype(lat_s.dtype))
        sum_s[half] = total
        acc_s[half] += jnp.dot(
            jnp.concatenate(pieces, axis=1),
            lat_s[keys, :width],
            preferred_element_type=jnp.float32,
        )

    def score(t):
        half, keys, offset = locate(t)
        s = lax.dot_general(
            q_ref[half], lat_s[keys, :], (((1,), (1,)), ((), ())), preferred_element_type=jnp.float32
        )
        row = lax.broadcasted_iota(jnp.int32, (rows, CHUNK), 0) % blk
        col = lax.broadcasted_iota(jnp.int32, (rows, CHUNK), 1)
        s = jnp.where(col - row <= offset, s, -1e30)
        sc_s[t] = s
        top = max_s[half]
        for j in range(CHUNK // LANES):
            top = jnp.maximum(top, s[:, j * LANES : (j + 1) * LANES])
        max_s[half] = top

    def run(*works):
        def body(t, _):
            for n in range(TURN):
                for work in works:
                    work(t * TURN + n)
            return 0

        def rest(t, _):
            for work in works:
                work(t)
            return 0

        lax.fori_loop(0, steps // TURN, body, 0)
        if steps % TURN:
            lax.fori_loop(steps - steps % TURN, steps, rest, 0)

    @pl.when(step > 0)
    def _():
        run(weigh)

    @pl.when(step < last)
    def _():
        run(score)

    @pl.when(step > 0)
    def _():
        for h in range(group):
            own = slice(h * blk, (h + 1) * blk)
            mixed = []
            for half in range(2):
                total = jnp.sum(sum_s[half, own], axis=1, keepdims=True)
                mixed.append((acc_s[half, own] / total).astype(lat_s.dtype))
                sum_s[half, own] = jnp.zeros((blk, LANES), jnp.float32)
                acc_s[half, own] = jnp.zeros((blk, width), jnp.float32)
            out_ref[:, h * value : (h + 1) * value] = jnp.dot(
                jnp.concatenate(mixed, axis=0), wuv_ref[h], preferred_element_type=jnp.float32
            ).astype(out_ref.dtype)

    for half in range(2):
        top_s[half] = jnp.broadcast_to(
            jnp.max(max_s[half], axis=1, keepdims=True), max_s.shape[1:]
        )
        max_s[half] = jnp.full(max_s.shape[1:], -1e30, jnp.float32)


def gather_kernel(
    sizes,
    lat_ref,
    qn_ref,
    qr_ref,
    wuk_ref,
    out_ref,
    query_ref,
    qn_s,
    qr_s,
    wuk_s,
    query_s,
    own_sem,
    send_sem,
    recv_sem,
    in_sem,
    out_sem,
):
    outer, inner, heads = sizes
    _, _, rows, padded = query_s.shape
    tok = qn_s.shape[0]
    blk = tok // 2
    total, nope, width = wuk_s.shape
    group = min(UNIT, total)
    parts = total // group
    share = rows // (group * blk)
    rope = qr_s.shape[1] // total
    loads = [
        pltpu.make_async_copy(qn_ref, qn_s, in_sem.at[parts]),
        pltpu.make_async_copy(qr_ref, qr_s, in_sem.at[parts + 1]),
    ]
    for g in range(parts):
        span = pl.ds(g * group, group)
        loads.append(pltpu.make_async_copy(wuk_ref.at[span], wuk_s.at[span], in_sem.at[g]))
    stores = []
    for g in range(parts):
        at = (g // share, slice(None), pl.ds((g % share) * group * blk, group * blk))
        stores.append(pltpu.make_async_copy(query_s.at[at], query_ref.at[at], out_sem.at[g]))

    def project(g):
        if g == 0:
            loads[0].wait()
            loads[1].wait()
        if g < parts:
            loads[2 + g].wait()

            def pair(p, _):
                turns = qr_s[:, pl.ds(pl.multiple_of((g * group + 2 * p) * rope, 2 * rope), 2 * rope)]
                for j in range(2):
                    h = 2 * p + j
                    head = g * group + h
                    own = jnp.dot(
                        qn_s[:, pl.ds(pl.multiple_of(head * nope, nope), nope)],
                        wuk_s[head],
                        preferred_element_type=jnp.float32,
                    ).astype(query_s.dtype)
                    turn = turns[:, j * rope : (j + 1) * rope]
                    fill = jnp.zeros((tok, padded - width - rope), turn.dtype)
                    tail = jnp.concatenate([turn, fill], axis=1)
                    for half in range(2):
                        cut = slice(half * blk, (half + 1) * blk)
                        to = pl.ds(pl.multiple_of(((g % share) * group + h) * blk, blk), blk)
                        query_s[g // share, half, to, :width] = own[cut]
                        query_s[g // share, half, to, width:] = tail[cut]
                return 0

            lax.fori_loop(0, group // 2, pair, 0)
        if 1 <= g <= parts:
            stores[g - 1].start()

    swap = inner == heads
    me, y = lax.axis_index("ctx"), lax.axis_index("head")
    core = me % 2
    z, x = (me // 2) // inner, (me // 2) % inner
    turned = core if swap else 0
    u, v = x + turned * (y - x), y + turned * (x - y)

    def coords(zz, uu, vv):
        return zz, uu + turned * (vv - uu), vv + turned * (uu - vv)

    def block(zz, uu, vv, cc):
        zz, xx, yy = coords(zz, uu, vv)
        return ((zz * inner + xx) * 2 + cc) * heads + yy

    def device(zz, uu, vv, cc):
        zz, xx, yy = coords(zz, uu, vv)
        return ((zz * inner + xx) * 2 + cc, yy)

    zs = [(z + d) % outer for d in range(outer)]
    us = [(u + d) % inner for d in range(inner)]
    vs = [(v + d) % heads for d in range(heads)]
    z_peers = [device(p, u, v, core) for p in zs[:0:-1]]
    u_peers = [device(z, p, v, core) for p in us[1:]]
    v_peers = [device(z, u, p, core) for p in vs[1:]]
    partner = [(z * inner * 2 + x * 2 + 1 - core, y)]
    everyone = z_peers + u_peers + v_peers + partner

    own = block(z, u, v, core)
    keep = pltpu.make_async_copy(lat_ref, out_ref.at[own], own_sem)
    keep.start()
    for load in loads:
        load.start()

    barrier = pltpu.get_barrier_semaphore()
    for peer in everyone:
        pl.semaphore_signal(barrier, inc=1, device_id=peer, device_id_type=MESH)
    pl.semaphore_wait(barrier, len(everyone))

    sent = []

    def send(src, b, peers):
        for peer in peers:
            copy = pltpu.make_async_remote_copy(
                src_ref=src,
                dst_ref=out_ref.at[b],
                send_sem=send_sem.at[len(sent)],
                recv_sem=recv_sem.at[b],
                device_id=peer,
                device_id_type=MESH,
            )
            copy.start()
            sent.append(copy)

    def arrive(b):
        pltpu.make_async_remote_copy(
            src_ref=out_ref.at[b],
            dst_ref=out_ref.at[b],
            send_sem=send_sem.at[0],
            recv_sem=recv_sem.at[b],
            device_id=partner[0],
            device_id_type=MESH,
        ).wait_recv()

    def relay(b, peers):
        arrive(b)
        send(out_ref.at[b], b, peers)

    send(lat_ref, own, u_peers + v_peers + z_peers + partner)
    route = [(block(z, uu, v, core), v_peers + partner) for uu in us[1:]]
    for d in range(1, outer + 1):
        if d < outer:
            route.append((block(zs[d], u, v, core), u_peers + v_peers + partner))
        if d > 1:
            route += [(block(zs[d - 1], uu, v, core), v_peers + partner) for uu in us[1:]]
    route += [(block(zz, u, vv, core), partner) for zz in zs for vv in vs[1:]]
    route += [
        (block(zz, uu, vv, core), partner) for zz in zs for uu in us[1:] for vv in vs[1:]
    ]
    project(0)
    project(1)
    for place, (b, peers) in enumerate(route):
        relay(b, peers)
        if place % 2:
            project(2 + place // 2)
    for g in range(2 + len(route) // 2, parts + 1):
        project(g)
    for zz in range(outer):
        for xx in range(inner):
            for yy in range(heads):
                arrive(((zz * inner + xx) * 2 + 1 - core) * heads + yy)
    for copy in sent:
        copy.wait_send()
    for store in stores:
        store.wait()
    keep.wait()


def gather(latent, q_nope, q_rope, w_uk, ctx, head_axis, group):
    chips = ctx // 2
    inner = 2 if chips % 2 == 0 else 1
    sizes = (chips // inner, inner, head_axis)
    shard, full = latent.shape
    blocks = ctx * head_axis
    heads, nope, width = w_uk.shape
    tok = q_nope.shape[0]
    rows = group * tok // 2
    parts = heads // group
    padded = -(-full // LANES) * LANES
    kind = latent.dtype
    lat, query = pl.pallas_call(
        functools.partial(gather_kernel, sizes),
        out_shape=(
            jax.ShapeDtypeStruct((blocks, shard, full), kind),
            jax.ShapeDtypeStruct((parts, 2, rows, padded), kind),
        ),
        in_specs=[
            pl.BlockSpec(memory_space=pltpu.VMEM),
            pl.BlockSpec(memory_space=pl.ANY),
            pl.BlockSpec(memory_space=pl.ANY),
            pl.BlockSpec(memory_space=pl.ANY),
        ],
        out_specs=(
            pl.BlockSpec(memory_space=pltpu.VMEM),
            pl.BlockSpec(memory_space=pl.ANY),
        ),
        scratch_shapes=[
            pltpu.VMEM(q_nope.shape, kind),
            pltpu.VMEM(q_rope.shape, kind),
            pltpu.VMEM(w_uk.shape, kind),
            pltpu.VMEM((parts, 2, rows, padded), kind),
            pltpu.SemaphoreType.DMA,
            pltpu.SemaphoreType.DMA((blocks,)),
            pltpu.SemaphoreType.DMA((blocks,)),
            pltpu.SemaphoreType.DMA((heads // min(UNIT, heads) + 2,)),
            pltpu.SemaphoreType.DMA((heads // min(UNIT, heads),)),
        ],
        compiler_params=pltpu.CompilerParams(collective_id=0, has_side_effects=True),
    )(latent, q_nope, q_rope, w_uk)
    return lat.reshape(blocks * shard, full), query


def attend(lat, query, starts, w_uv, scale2, group):
    heads, width, value = w_uv.shape
    parts, _, rows, padded = query.shape
    blk = rows // group
    seq = lat.shape[0]
    steps = seq // CHUNK + 1
    return pl.pallas_call(
        functools.partial(attention_kernel, scale2, blk),
        grid=(parts + 1,),
        out_shape=jax.ShapeDtypeStruct((2 * blk, heads * value), lat.dtype),
        in_specs=[
            pl.BlockSpec(memory_space=pltpu.SMEM),
            pl.BlockSpec(memory_space=pltpu.VMEM),
            pl.BlockSpec((None, 2, rows, padded), lambda i: (jnp.minimum(i, parts - 1), 0, 0, 0)),
            pl.BlockSpec((group, width, value), lambda i: (jnp.maximum(i - 1, 0), 0, 0)),
        ],
        out_specs=pl.BlockSpec((2 * blk, group * value), lambda i: (0, jnp.maximum(i - 1, 0))),
        scratch_shapes=[
            pltpu.VMEM((seq, padded), lat.dtype),
            pltpu.VMEM((steps, rows, CHUNK), jnp.float32),
            pltpu.VMEM((2, rows, width), jnp.float32),
            pltpu.VMEM((2, rows, LANES), jnp.float32),
            pltpu.VMEM((2, rows, LANES), jnp.float32),
            pltpu.VMEM((2, rows, LANES), jnp.float32),
        ],
        compiler_params=pltpu.CompilerParams(dimension_semantics=("arbitrary",)),
    )(starts, lat, query, w_uv)


def shards(sizes, q_nope, q_rope, latent, block_start, w_uk, w_uv):
    group = min(GROUP, w_uk.shape[0])
    rope = q_rope.shape[1] // w_uk.shape[0]
    scale2 = math.log2(math.e) / math.sqrt(w_uk.shape[1] + rope)
    lat, query = gather(latent, q_nope, q_rope, w_uk, *sizes, group)
    return attend(lat, query, block_start, w_uv, scale2, group)


def solution(mesh):
    placed = (
        P("ctx", "head"),
        P("ctx", "head"),
        P(("ctx", "head"), None),
        P(),
        P("head", None, None),
        P("head", None, None),
    )
    sizes = (mesh.shape["ctx"], mesh.shape["head"])
    return jax.shard_map(
        functools.partial(shards, sizes), mesh=mesh, in_specs=placed, out_specs=P("ctx", "head"), check_vma=False
    )
```

```python
import functools
import math

import jax
import jax.numpy as jnp
from jax import lax
from jax.experimental import pallas as pl
from jax.experimental.pallas import tpu as pltpu
from jax.sharding import PartitionSpec as P

CHUNK = 256
LANES = 128
GROUP = 16
UNIT = 8
TURN = 9
MESH = pl.DeviceIdType.MESH


def attention_kernel(
    scale2,
    blk,
    starts_ref,
    lat_ref,
    q_ref,
    wuv_ref,
    out_ref,
    lat_s,
    sc_s,
    acc_s,
    max_s,
    top_s,
    sum_s,
):
    group, width, value = wuv_ref.shape
    rows = group * blk
    seq, full = lat_ref.shape
    steps = seq // CHUNK + 1
    padded = lat_s.shape[1]
    me = lax.axis_index("ctx")
    start_a = starts_ref[2 * me]
    start_b = starts_ref[2 * me + 1]
    count_a = start_a // CHUNK + 1
    step = pl.program_id(0)
    last = pl.num_programs(0) - 1

    @pl.when(step == 0)
    def _():
        max_s[...] = jnp.full(max_s.shape, -1e30, jnp.float32)
        sum_s[...] = jnp.zeros(sum_s.shape, jnp.float32)
        acc_s[...] = jnp.zeros(acc_s.shape, jnp.float32)

        def place(b, _):
            src = pl.ds(pl.multiple_of(b * blk, blk), blk)
            dst = pl.ds(pl.multiple_of(starts_ref[b], blk), blk)
            lat_s[dst, :width] = lat_ref[src, :width]
            tail = lat_ref[src, width:]
            fill = jnp.zeros((blk, padded - full), tail.dtype)
            lat_s[dst, width:] = jnp.concatenate([tail, fill], axis=1)
            return 0

        lax.fori_loop(0, seq // blk, place, 0)

    def locate(t):
        upper = t >= count_a
        half = jnp.where(upper, 1, 0)
        chunk = jnp.where(upper, t - count_a, t)
        offset = jnp.where(upper, start_b, start_a) - chunk * CHUNK
        return half, pl.ds(pl.multiple_of(chunk * CHUNK, CHUNK), CHUNK), offset

    def weigh(t):
        half, keys, _ = locate(t)
        top = top_s[half]
        total = sum_s[half]
        pieces = []
        for j in range(CHUNK // LANES):
            w = jnp.exp2((sc_s[t, :, j * LANES : (j + 1) * LANES] - top) * scale2)
            total = total + w
            pieces.append(w.astype(lat_s.dtype))
        sum_s[half] = total
        acc_s[half] += jnp.dot(
            jnp.concatenate(pieces, axis=1),
            lat_s[keys, :width],
            preferred_element_type=jnp.float32,
        )

    def score(t):
        half, keys, offset = locate(t)
        s = lax.dot_general(
            q_ref[half], lat_s[keys, :], (((1,), (1,)), ((), ())), preferred_element_type=jnp.float32
        )
        row = lax.broadcasted_iota(jnp.int32, (rows, CHUNK), 0) % blk
        col = lax.broadcasted_iota(jnp.int32, (rows, CHUNK), 1)
        s = jnp.where(col - row <= offset, s, -1e30)
        sc_s[t] = s
        top = max_s[half]
        for j in range(CHUNK // LANES):
            top = jnp.maximum(top, s[:, j * LANES : (j + 1) * LANES])
        max_s[half] = top

    def run(*works):
        def body(t, _):
            for n in range(TURN):
                for work in works:
                    work(t * TURN + n)
            return 0

        def rest(t, _):
            for work in works:
                work(t)
            return 0

        lax.fori_loop(0, steps // TURN, body, 0)
        if steps % TURN:
            lax.fori_loop(steps - steps % TURN, steps, rest, 0)

    @pl.when(step > 0)
    def _():
        run(weigh)

    @pl.when(step < last)
    def _():
        run(score)

    @pl.when(step > 0)
    def _():
        for h in range(group):
            own = slice(h * blk, (h + 1) * blk)
            mixed = []
            for half in range(2):
                total = jnp.sum(sum_s[half, own], axis=1, keepdims=True)
                mixed.append((acc_s[half, own] / total).astype(lat_s.dtype))
                sum_s[half, own] = jnp.zeros((blk, LANES), jnp.float32)
                acc_s[half, own] = jnp.zeros((blk, width), jnp.float32)
            out_ref[:, h * value : (h + 1) * value] = jnp.dot(
                jnp.concatenate(mixed, axis=0), wuv_ref[h], preferred_element_type=jnp.float32
            ).astype(out_ref.dtype)

    @pl.when(step < last)
    def _():
        for half in range(2):
            top_s[half] = jnp.broadcast_to(
                jnp.max(max_s[half], axis=1, keepdims=True), max_s.shape[1:]
            )
            max_s[half] = jnp.full(max_s.shape[1:], -1e30, jnp.float32)


def gather_kernel(
    sizes,
    lat_ref,
    qn_ref,
    qr_ref,
    wuk_ref,
    out_ref,
    query_ref,
    qn_s,
    qr_s,
    wuk_s,
    query_s,
    own_sem,
    send_sem,
    recv_sem,
    in_sem,
    out_sem,
):
    outer, inner, heads = sizes
    _, _, rows, padded = query_s.shape
    tok = qn_s.shape[0]
    blk = tok // 2
    total, nope, width = wuk_s.shape
    group = min(UNIT, total)
    parts = total // group
    share = rows // (group * blk)
    rope = qr_s.shape[1] // total
    loads = [
        pltpu.make_async_copy(qn_ref, qn_s, in_sem.at[parts]),
        pltpu.make_async_copy(qr_ref, qr_s, in_sem.at[parts + 1]),
    ]
    for g in range(parts):
        span = pl.ds(g * group, group)
        loads.append(pltpu.make_async_copy(wuk_ref.at[span], wuk_s.at[span], in_sem.at[g]))
    stores = []
    for g in range(parts):
        at = (g // share, slice(None), pl.ds((g % share) * group * blk, group * blk))
        stores.append(pltpu.make_async_copy(query_s.at[at], query_ref.at[at], out_sem.at[g]))

    def project(g):
        if g == 0:
            loads[0].wait()
            loads[1].wait()
        if g < parts:
            loads[2 + g].wait()

            def pair(p, _):
                turns = qr_s[:, pl.ds(pl.multiple_of((g * group + 2 * p) * rope, 2 * rope), 2 * rope)]
                for j in range(2):
                    h = 2 * p + j
                    head = g * group + h
                    own = jnp.dot(
                        qn_s[:, pl.ds(pl.multiple_of(head * nope, nope), nope)],
                        wuk_s[head],
                        preferred_element_type=jnp.float32,
                    ).astype(query_s.dtype)
                    turn = turns[:, j * rope : (j + 1) * rope]
                    fill = jnp.zeros((tok, padded - width - rope), turn.dtype)
                    tail = jnp.concatenate([turn, fill], axis=1)
                    for half in range(2):
                        cut = slice(half * blk, (half + 1) * blk)
                        to = pl.ds(pl.multiple_of(((g % share) * group + h) * blk, blk), blk)
                        query_s[g // share, half, to, :width] = own[cut]
                        query_s[g // share, half, to, width:] = tail[cut]
                return 0

            lax.fori_loop(0, group // 2, pair, 0)
        if 1 <= g <= parts:
            stores[g - 1].start()

    swap = inner == heads
    me, y = lax.axis_index("ctx"), lax.axis_index("head")
    core = me % 2
    z, x = (me // 2) // inner, (me // 2) % inner
    turned = core if swap else 0
    u, v = x + turned * (y - x), y + turned * (x - y)

    def coords(zz, uu, vv):
        return zz, uu + turned * (vv - uu), vv + turned * (uu - vv)

    def block(zz, uu, vv, cc):
        zz, xx, yy = coords(zz, uu, vv)
        return ((zz * inner + xx) * 2 + cc) * heads + yy

    def device(zz, uu, vv, cc):
        zz, xx, yy = coords(zz, uu, vv)
        return ((zz * inner + xx) * 2 + cc, yy)

    zs = [(z + d) % outer for d in range(outer)]
    us = [(u + d) % inner for d in range(inner)]
    vs = [(v + d) % heads for d in range(heads)]
    z_peers = [device(p, u, v, core) for p in zs[:0:-1]]
    u_peers = [device(z, p, v, core) for p in us[1:]]
    v_peers = [device(z, u, p, core) for p in vs[1:]]
    partner = [(z * inner * 2 + x * 2 + 1 - core, y)]
    everyone = z_peers + u_peers + v_peers + partner

    own = block(z, u, v, core)
    keep = pltpu.make_async_copy(lat_ref, out_ref.at[own], own_sem)
    keep.start()
    for load in loads:
        load.start()

    barrier = pltpu.get_barrier_semaphore()
    for peer in everyone:
        pl.semaphore_signal(barrier, inc=1, device_id=peer, device_id_type=MESH)
    pl.semaphore_wait(barrier, len(everyone))

    sent = []

    def send(src, b, peers):
        for peer in peers:
            copy = pltpu.make_async_remote_copy(
                src_ref=src,
                dst_ref=out_ref.at[b],
                send_sem=send_sem.at[len(sent)],
                recv_sem=recv_sem.at[b],
                device_id=peer,
                device_id_type=MESH,
            )
            copy.start()
            sent.append(copy)

    def arrive(b):
        pltpu.make_async_remote_copy(
            src_ref=out_ref.at[b],
            dst_ref=out_ref.at[b],
            send_sem=send_sem.at[0],
            recv_sem=recv_sem.at[b],
            device_id=partner[0],
            device_id_type=MESH,
        ).wait_recv()

    def relay(b, peers):
        arrive(b)
        send(out_ref.at[b], b, peers)

    send(lat_ref, own, u_peers + v_peers + z_peers + partner)
    route = [(block(z, uu, v, core), v_peers + partner) for uu in us[1:]]
    for d in range(1, outer + 1):
        if d < outer:
            route.append((block(zs[d], u, v, core), u_peers + v_peers + partner))
        if d > 1:
            route += [(block(zs[d - 1], uu, v, core), v_peers + partner) for uu in us[1:]]
    route += [(block(zz, u, vv, core), partner) for zz in zs for vv in vs[1:]]
    route += [
        (block(zz, uu, vv, core), partner) for zz in zs for uu in us[1:] for vv in vs[1:]
    ]
    project(0)
    project(1)
    for place, (b, peers) in enumerate(route):
        relay(b, peers)
        if place % 2:
            project(2 + place // 2)
    for g in range(2 + len(route) // 2, parts + 1):
        project(g)
    for zz in range(outer):
        for xx in range(inner):
            for yy in range(heads):
                arrive(((zz * inner + xx) * 2 + 1 - core) * heads + yy)
    for copy in sent:
        copy.wait_send()
    for store in stores:
        store.wait()
    keep.wait()


def gather(latent, q_nope, q_rope, w_uk, ctx, head_axis, group):
    chips = ctx // 2
    inner = 2 if chips % 2 == 0 else 1
    sizes = (chips // inner, inner, head_axis)
    shard, full = latent.shape
    blocks = ctx * head_axis
    heads, nope, width = w_uk.shape
    tok = q_nope.shape[0]
    rows = group * tok // 2
    parts = heads // group
    padded = -(-full // LANES) * LANES
    kind = latent.dtype
    lat, query = pl.pallas_call(
        functools.partial(gather_kernel, sizes),
        out_shape=(
            jax.ShapeDtypeStruct((blocks, shard, full), kind),
            jax.ShapeDtypeStruct((parts, 2, rows, padded), kind),
        ),
        in_specs=[
            pl.BlockSpec(memory_space=pltpu.VMEM),
            pl.BlockSpec(memory_space=pl.ANY),
            pl.BlockSpec(memory_space=pl.ANY),
            pl.BlockSpec(memory_space=pl.ANY),
        ],
        out_specs=(
            pl.BlockSpec(memory_space=pltpu.VMEM),
            pl.BlockSpec(memory_space=pl.ANY),
        ),
        scratch_shapes=[
            pltpu.VMEM(q_nope.shape, kind),
            pltpu.VMEM(q_rope.shape, kind),
            pltpu.VMEM(w_uk.shape, kind),
            pltpu.VMEM((parts, 2, rows, padded), kind),
            pltpu.SemaphoreType.DMA,
            pltpu.SemaphoreType.DMA((blocks,)),
            pltpu.SemaphoreType.DMA((blocks,)),
            pltpu.SemaphoreType.DMA((heads // min(UNIT, heads) + 2,)),
            pltpu.SemaphoreType.DMA((heads // min(UNIT, heads),)),
        ],
        compiler_params=pltpu.CompilerParams(collective_id=0, has_side_effects=True),
    )(latent, q_nope, q_rope, w_uk)
    return lat.reshape(blocks * shard, full), query


def attend(lat, query, starts, w_uv, scale2, group):
    heads, width, value = w_uv.shape
    parts, _, rows, padded = query.shape
    blk = rows // group
    seq = lat.shape[0]
    steps = seq // CHUNK + 1
    return pl.pallas_call(
        functools.partial(attention_kernel, scale2, blk),
        grid=(parts + 1,),
        out_shape=jax.ShapeDtypeStruct((2 * blk, heads * value), lat.dtype),
        in_specs=[
            pl.BlockSpec(memory_space=pltpu.SMEM),
            pl.BlockSpec(memory_space=pltpu.VMEM),
            pl.BlockSpec((None, 2, rows, padded), lambda i: (jnp.minimum(i, parts - 1), 0, 0, 0)),
            pl.BlockSpec((group, width, value), lambda i: (jnp.maximum(i - 1, 0), 0, 0)),
        ],
        out_specs=pl.BlockSpec((2 * blk, group * value), lambda i: (0, jnp.maximum(i - 1, 0))),
        scratch_shapes=[
            pltpu.VMEM((seq, padded), lat.dtype),
            pltpu.VMEM((steps, rows, CHUNK), jnp.float32),
            pltpu.VMEM((2, rows, width), jnp.float32),
            pltpu.VMEM((2, rows, LANES), jnp.float32),
            pltpu.VMEM((2, rows, LANES), jnp.float32),
            pltpu.VMEM((2, rows, LANES), jnp.float32),
        ],
        compiler_params=pltpu.CompilerParams(dimension_semantics=("arbitrary",)),
    )(starts, lat, query, w_uv)


def shards(sizes, q_nope, q_rope, latent, block_start, w_uk, w_uv):
    group = min(GROUP, w_uk.shape[0])
    rope = q_rope.shape[1] // w_uk.shape[0]
    scale2 = math.log2(math.e) / math.sqrt(w_uk.shape[1] + rope)
    lat, query = gather(latent, q_nope, q_rope, w_uk, *sizes, group)
    return attend(lat, query, block_start, w_uv, scale2, group)


def solution(mesh):
    placed = (
        P("ctx", "head"),
        P("ctx", "head"),
        P(("ctx", "head"), None),
        P(),
        P("head", None, None),
        P("head", None, None),
    )
    sizes = (mesh.shape["ctx"], mesh.shape["head"])
    return jax.shard_map(
        functools.partial(shards, sizes), mesh=mesh, in_specs=placed, out_specs=P("ctx", "head"), check_vma=False
    )
```
